32 devices in a mesh: row: 8 (over y, x, core), col: 4 (over z).
Axes of the slice: x: 2, y: 2, z: 4, core: 2. Of those that a mesh axis runs over, the one named last changes fastest.
Arguments:
- positions: float32 [3, 32768], P(None, ('row', 'col')), may hold values from -1 to 1
- normals: float32 [3, 32768], P(None, ('row', 'col')), may hold values from -4 to 4
- areas: float32 [32768], P(('row', 'col')), may hold values from 0.00012207031 to 0.0012207031
- direct: bfloat16 [32768, 64], P(('row', 'col')), may hold values from -6 to 6
- adjoint: bfloat16 [32768, 64], P(('row', 'col')), may hold values from -6 to 6
- spline: bfloat16 [32, 256, 512], P(('row', 'col')), may hold values from -0.375 to 0.375
- block_lists: int32 [128, 4], replicated, may hold values from 0 to 31, all different within a row
- patch_counts: int32 [64], replicated, may hold values from 1 to 8, 128 in all
- patch_owner: int32 [64], replicated, may hold values from 0 to 63, each once
Outputs:
- densities: float32 [32768], P(('row', 'col'))
- patch_grad: float32 [64, 512], P('row')
The draws below stay inside these ranges and needn't reach their ends.
Inputs may be any that keep to these rules, and one draw needn't show every extreme that they name: `block_lists`: each row names 4 different spline blocks, and every spline block is named by some row. `patch_counts`: the counts sum to 128; the largest is exactly 8. `patch_owner`: A permutation of the patches.
All inputs are finite; a program needn't handle non-finite values.
Results may differ from the reference program's by a relative error of at most 0.0029.
Values may be sent and summed in bfloat16 or wider, within the bound.
A program may use at most 64 MiB of HBM per device.

```python
import math
import jax
import jax.numpy as jnp
import numpy as np
from jax import lax

P_SIZE = 32768
H = 32
BPAN = 256
CTRL = 512
LISTS = 4
NPATCH = 64
MOSTB = 8
NBLK = 128
NSPL = 32
COLS = 64


def block_scale(rng, extent, cuts, least, high):
    gain = 1.0
    for dim, blocks in cuts:
        draws = jax.random.uniform(jax.random.fold_in(jax.random.fold_in(rng, 6), dim), (blocks,), jnp.float32, least / len(cuts), high / len(cuts))
        gain = gain * jnp.repeat(jnp.exp(draws), extent[dim] // blocks).reshape((-1,) + (1,) * (len(extent) - 1 - dim))
    return gain


def picks_of(stream_key, rows, count, top, lift):
    order = jax.random.permutation(jax.random.fold_in(stream_key, 1), count)
    favour = order
    for power in range(3):
        favour = favour * favour // count
    favour = favour * lift // count
    chance = jax.random.randint(jax.random.fold_in(stream_key, 2), (rows, count), 0, 4096) + favour
    sure = jax.random.permutation(jax.random.fold_in(stream_key, 3), rows)[jnp.arange(count) % rows]
    chance = jnp.where(jnp.arange(rows)[:, None] == sure[None, :], 1 << 14, chance)
    priority = chance * count + jnp.arange(count)
    return lax.top_k(priority.astype(jnp.int32), top)[1].astype(jnp.int32)


def split_up(amount, total, limit, lean):
    loads = [(1 << 20) // math.isqrt(rank ** lean) + 1 for rank in range(2, amount + 1)]
    rest, given = total - limit - (amount - 1), [1] * (amount - 1)
    while rest > 0:
        movable = [i for i in range(amount - 1) if given[i] < limit]
        mass, remaining = sum([loads[i] for i in movable]), rest
        for i in movable:
            addition = min(limit - given[i], max(1, remaining * loads[i] // mass), rest)
            given[i] = given[i] + addition
            rest = rest - addition
    return np.array([limit] + given)


def ragged(stream_key, number_of, total, most, skew):
    if number_of == 2:
        one = jax.random.randint(stream_key, (), max(1, total - most), min(most, total - 1) + 1)
        return jnp.stack([one, total - one])
    lengths = jnp.asarray(split_up(number_of, total, most, skew), jnp.int32)
    pairs = (number_of - 1) // 2
    donor, receiver = lengths[1:1 + 2 * pairs:2], lengths[2:2 + 2 * pairs:2]
    room = jnp.minimum(donor - 1, most - receiver)
    moved = jax.random.randint(jax.random.fold_in(stream_key, 1), (pairs,), 0, 1 << 20) % (room + 1)
    lengths = lengths.at[1:1 + 2 * pairs:2].set(donor - moved).at[2:2 + 2 * pairs:2].set(receiver + moved)
    return lengths[jax.random.permutation(jax.random.fold_in(stream_key, 2), number_of)]


def bell_draw(rng, shape, width, most, split=(), kind=jnp.bfloat16):
    loudness = block_scale(rng, shape, split, -0.22, 0.18) if split else 1.0
    drawn = jax.random.normal(rng, shape, jnp.float32) * width * loudness
    return jnp.minimum(jnp.maximum(drawn, -most), most).astype(kind)


def setup_inputs(seed: int = 0) -> dict:
    seeds = jax.random.split(jax.random.key(seed), 10)
    positions = jnp.clip(jax.random.uniform(seeds[0], (3, P_SIZE), jnp.float32, -1.0, 1.0) * block_scale(seeds[0], (3, P_SIZE), ((1, 32),), -0.4, 0.0), -1.0, 1.0)
    normals = bell_draw(seeds[1], (3, P_SIZE), 1.0, 4.0, ((1, 32),), jnp.float32)
    areas = jnp.clip(jnp.exp(math.log(0.0012207031) - 2.3025851 * jax.random.uniform(seeds[2], (P_SIZE,), jnp.float32) ** block_scale(seeds[2], (P_SIZE,), ((0, 32),), -0.2, 0.2)), 0.00012207031, 0.0012207031)
    direct = bell_draw(seeds[3], (P_SIZE, COLS), 1.0, 6.0, ((0, 32),))
    adjoint = bell_draw(seeds[4], (P_SIZE, COLS), 1.0, 6.0, ((0, 32),))
    spline = bell_draw(seeds[5], (NSPL, BPAN, CTRL), BPAN ** -0.5, 0.375, ((0, 32),))
    block_lists = picks_of(seeds[6], NBLK, NSPL, LISTS, 2048)
    patch_counts = ragged(seeds[7], NPATCH, NBLK, MOSTB, 2).astype(jnp.int32)
    patch_owner = jax.random.permutation(seeds[8], NPATCH).astype(jnp.int32)
    return dict(positions=positions, normals=normals, areas=areas, direct=direct, adjoint=adjoint, spline=spline, block_lists=block_lists, patch_counts=patch_counts, patch_owner=patch_owner)


wave_number = 6.0
inv_four_pi = 0.07957747154594767

def kernel_block(tgt_pos, tgt_nrm, src_pos, src_area):
    depth_t = 0.5 * (tgt_pos[2] - 1.2)
    depth_s = 0.5 * (src_pos[2] - 1.2)
    delta_x = tgt_pos[0][:, None] - src_pos[0][None, :]
    delta_y = tgt_pos[1][:, None] - src_pos[1][None, :]
    delta_z = depth_t[:, None] - depth_s[None, :]
    image_z = depth_t[:, None] + depth_s[None, :]
    area_row = src_area[None, :]
    level = delta_x * delta_x + delta_y * delta_y
    near = level + delta_z * delta_z + area_row
    mirror = level + image_z * image_z + area_row
    slope = tgt_nrm[0][:, None] * delta_x + tgt_nrm[1][:, None] * delta_y
    vertical = tgt_nrm[2][:, None]
    rankine = (slope + vertical * delta_z) / (near * jnp.sqrt(near))
    reflect = (slope + vertical * image_z) / (mirror * jnp.sqrt(mirror))
    waves = 2.0 * wave_number * jnp.exp(wave_number * image_z) * vertical * jnp.cos(wave_number * jnp.sqrt(level + area_row))
    return area_row * (rankine + reflect - waves) * inv_four_pi

def reference(positions, normals, areas, direct, adjoint, spline, block_lists, patch_counts, patch_owner):
    step_rows = min(P_SIZE, 256)
    count = P_SIZE // step_rows

    def advance(carry, index):
        start = (index * step_rows).astype(jnp.int32)
        tgt_pos = lax.dynamic_slice_in_dim(positions, start, step_rows, 1)
        tgt_nrm = lax.dynamic_slice_in_dim(normals, start, step_rows, 1)
        adj_rows = lax.dynamic_slice_in_dim(adjoint, start, step_rows, 0)
        tile = kernel_block(tgt_pos, tgt_nrm, positions, areas).astype(jnp.bfloat16)
        image_rows = jnp.dot(tile, direct, preferred_element_type=jnp.float32)
        carry = carry + lax.dot_general(tile, adj_rows, (((0,), (0,)), ((), ())), preferred_element_type=jnp.float32)
        return (carry, image_rows)
    adjoint_image, pieces = lax.scan(advance, jnp.zeros((P_SIZE, 2 * H), jnp.float32), jnp.arange(count, dtype=jnp.int32))
    direct_image = pieces.reshape(P_SIZE, 2 * H)
    densities = lax.optimization_barrier(jnp.sum(adjoint.astype(jnp.float32) * direct_image + direct.astype(jnp.float32) * adjoint_image, axis=1))
    blocks = densities.reshape(NBLK, BPAN)

    def one_block(item):
        values, listed = item
        basis = lax.optimization_barrier(jnp.sum(spline[listed].astype(jnp.float32), axis=0))
        return jnp.dot(values, basis, precision=lax.Precision.HIGHEST)
    block_grad = lax.map(one_block, (blocks, block_lists))
    ends = jnp.cumsum(patch_counts).astype(jnp.int32)
    starts = ends - patch_counts
    block_ids = jnp.arange(NBLK, dtype=jnp.int32)
    inside = ((starts[:, None] <= block_ids[None, :]) & (block_ids[None, :] < ends[:, None])).astype(jnp.float32)
    owners = (patch_owner[None, :] == jnp.arange(NPATCH, dtype=jnp.int32)[:, None]).astype(jnp.float32)
    owned = jnp.dot(owners, inside, precision=lax.Precision.HIGHEST)
    patch_grad = jnp.dot(owned, block_grad, precision=lax.Precision.HIGHEST)
    return (densities, patch_grad)
```

```python
import functools
import math

import jax
import jax.numpy as jnp
from jax import lax
from jax.experimental import pallas as pl
from jax.experimental.pallas import tpu as pltpu
from jax.sharding import PartitionSpec as P

BPAN = 256
NPATCH = 64
NBLK = 128

wave_number = 6.0
inv_four_pi = 0.07957747154594767

HALF_ANGLE = (
    0.5624999387637301,
    -0.026367050589663217,
    0.0004942961270241117,
    -4.941951390951122e-06,
    2.8141817781696455e-08,
)
SQ_SCALE = HALF_ANGLE[-1] ** (1.0 / len(HALF_ANGLE))
MONIC = tuple(c / SQ_SCALE ** (i + 1) for i, c in enumerate(HALF_ANGLE[:-1]))

T_FIELDS = 7
S_FIELDS = 8


def pair_kernel(step_rows, tgt_ref, src_ref, adj_ref, dir_ref, image_ref, adjoint_ref, tile_ref):
    j = pl.program_id(0)
    i = pl.program_id(1)
    rows_here, lanes_here = tile_ref.shape
    for start in range(0, rows_here, step_rows):
        rows = pl.ds(start, step_rows)

        def column(field):
            return tgt_ref[rows, field : field + 1]

        def row(field):
            full = src_ref[8 * field : 8 * field + 8, :]
            return jnp.concatenate([full] * (step_rows // 8), axis=0)

        tx, ty, tz, nx, ny, nz, tw = [column(f) for f in range(T_FIELDS)]
        sx, sy, sz, sz4, sz2, sa, se, sk = [row(f) for f in range(S_FIELDS)]
        delta_x = tx - sx
        delta_y = ty - sy
        delta_z = tz - sz
        level = delta_x * delta_x + delta_y * delta_y + sa
        near = level + delta_z * delta_z
        mirror = near + tz * sz4
        r_near = lax.rsqrt(near)
        r_mirror = lax.rsqrt(mirror)
        facing = nx * delta_x + ny * delta_y + nz * delta_z
        facing_mirror = facing + nz * sz2
        arc = level + MONIC[3]
        arc = arc * level + MONIC[2]
        arc = arc * level + MONIC[1]
        arc = arc * level + MONIC[0]
        arc = arc * level
        arc = arc * (4.0 - arc)
        arc = arc * (4.0 - arc)
        arc = arc * (4.0 - arc)
        total = (
            facing * (r_near * r_near * r_near)
            + facing_mirror * (r_mirror * r_mirror * r_mirror)
            + (arc - 2.0) * (tw * se)
        )
        tile_ref[rows, :] = (total * sk).astype(jnp.bfloat16)

    tile = tile_ref[...]
    image = jnp.dot(tile, dir_ref[...], preferred_element_type=jnp.float32)
    back = jnp.dot(adj_ref[...], tile, preferred_element_type=jnp.float32)
    out_rows = pl.ds(pl.multiple_of(i * rows_here, rows_here), rows_here)

    @pl.when(j == 0)
    def _():
        image_ref[out_rows, :] = image

    @pl.when(j > 0)
    def _():
        image_ref[out_rows, :] += image

    @pl.when(i == 0)
    def _():
        adjoint_ref[...] = back

    @pl.when(i > 0)
    def _():
        adjoint_ref[...] += back


def pair_images(tgt, src, adj_cols, dir_src):
    targets = tgt.shape[0]
    sources = src.shape[1]
    columns = dir_src.shape[1]
    rows_here = min(targets, 256)
    lanes_here = min(sources, 512)
    return pl.pallas_call(
        functools.partial(pair_kernel, 16),
        grid=(sources // lanes_here, targets // rows_here),
        in_specs=[
            pl.BlockSpec((rows_here, tgt.shape[1]), lambda j, i: (i, 0)),
            pl.BlockSpec((src.shape[0], lanes_here), lambda j, i: (0, j)),
            pl.BlockSpec((columns, rows_here), lambda j, i: (0, i)),
            pl.BlockSpec((lanes_here, columns), lambda j, i: (j, 0)),
        ],
        out_specs=[
            pl.BlockSpec((targets, columns), lambda j, i: (0, 0)),
            pl.BlockSpec((columns, lanes_here), lambda j, i: (0, j)),
        ],
        out_shape=[
            jax.ShapeDtypeStruct((targets, columns), jnp.float32),
            jax.ShapeDtypeStruct((columns, sources), jnp.float32),
        ],
        scratch_shapes=[pltpu.VMEM((rows_here, lanes_here), jnp.bfloat16)],
        name="pair_images",
    )(tgt, src, adj_cols, dir_src)


def on_device(
    positions, normals, areas, direct, adjoint, spline, block_lists, patch_counts, patch_owner
):
    length = math.sqrt(SQ_SCALE)
    depth = 0.5 * (positions[2] - 1.2)
    grow = jnp.exp(wave_number * depth)
    flat = length * positions[:2]
    deep = (length * depth)[None]
    tgt_fields = jnp.concatenate(
        [
            flat,
            deep,
            normals,
            ((wave_number / SQ_SCALE) * normals[2] * grow)[None],
        ],
        axis=0,
    )
    src_fields = jnp.concatenate(
        [flat, deep, (SQ_SCALE * areas)[None], grow[None], ((SQ_SCALE * inv_four_pi) * areas)[None]],
        axis=0,
    )
    tgt_all = lax.all_gather(tgt_fields, "col", axis=1, tiled=True)
    src_all = lax.all_gather(src_fields, "row", axis=1, tiled=True)
    adj_tgt = lax.all_gather(adjoint, "col", axis=0, tiled=True)
    dir_src = lax.all_gather(direct, "row", axis=0, tiled=True)
    tgt = jnp.pad(tgt_all.T, ((0, 0), (0, 8 - T_FIELDS)))
    sz = src_all[2:3]
    src = jnp.repeat(
        jnp.concatenate([src_all[:3], 4.0 * sz, 2.0 * sz, src_all[3:]], axis=0), 8, axis=0
    )
    image, back = pair_images(tgt, src, adj_tgt.T, dir_src)
    dens_tgt = jnp.sum(adj_tgt.astype(jnp.float32) * image, axis=1)
    dens_src = jnp.sum(dir_src.T.astype(jnp.float32) * back, axis=0)
    densities = lax.psum_scatter(
        dens_tgt, "col", scatter_dimension=0, tiled=True
    ) + lax.psum_scatter(dens_src, "row", scatter_dimension=0, tiled=True)
    every_density = lax.all_gather(densities, ("row", "col"), axis=0, tiled=True)
    blocks = every_density.reshape(NBLK, BPAN)
    ends = jnp.cumsum(patch_counts)
    starts = ends - patch_counts
    block_ids = jnp.arange(NBLK, dtype=jnp.int32)
    inside = (
        (starts[:, None] <= block_ids[None, :]) & (block_ids[None, :] < ends[:, None])
    ).astype(jnp.float32)
    owners = (patch_owner[None, :] == jnp.arange(NPATCH, dtype=jnp.int32)[:, None]).astype(
        jnp.float32
    )
    owned = jnp.dot(owners, inside, precision=lax.Precision.HIGHEST)
    holder = lax.axis_index(("row", "col"))
    listed = jnp.any(block_lists == holder, axis=1).astype(jnp.float32)
    weights = owned * listed[None, :]
    gathered = jnp.dot(weights, blocks, precision=lax.Precision.HIGHEST)
    contrib = jnp.dot(gathered, spline[0].astype(jnp.float32), precision=lax.Precision.HIGHEST)
    partial_rows = lax.psum_scatter(contrib, "row", scatter_dimension=0, tiled=True)
    patch_grad = lax.psum(partial_rows, "col")
    return (densities, patch_grad)


def solution(mesh):
    placed = (
        P(None, ("row", "col")),
        P(None, ("row", "col")),
        P(("row", "col")),
        P(("row", "col"), None),
        P(("row", "col"), None),
        P(("row", "col"), None, None),
        P(),
        P(),
        P(),
    )
    return jax.shard_map(
        on_device,
        mesh=mesh,
        in_specs=placed,
        out_specs=(P(("row", "col")), P("row", None)),
        check_vma=False,
    )
```

```python
import functools
import math

import jax
import jax.numpy as jnp
from jax import lax
from jax.experimental import pallas as pl
from jax.experimental.pallas import tpu as pltpu
from jax.sharding import PartitionSpec as P

BPAN = 256
NPATCH = 64
NBLK = 128

wave_number = 6.0
inv_four_pi = 0.07957747154594767

HALF_ANGLE = (
    0.5624999387637301,
    -0.026367050589663217,
    0.0004942961270241117,
    -4.941951390951122e-06,
    2.8141817781696455e-08,
)
SQ_SCALE = HALF_ANGLE[-1] ** (1.0 / len(HALF_ANGLE))
MONIC = tuple(c / SQ_SCALE ** (i + 1) for i, c in enumerate(HALF_ANGLE[:-1]))

T_FIELDS = 7
S_FIELDS = 8


def pair_kernel(step_rows, tgt_ref, src_ref, adj_ref, dir_ref, image_ref, adjoint_ref, tile_ref):
    j = pl.program_id(0)
    i = pl.program_id(1)
    rows_here, lanes_here = tile_ref.shape
    for start in range(0, rows_here, step_rows):
        rows = pl.ds(start, step_rows)

        def column(field):
            return tgt_ref[rows, field : field + 1]

        def row(field):
            full = src_ref[8 * field : 8 * field + 8, :]
            return jnp.concatenate([full] * (step_rows // 8), axis=0)

        tx, ty, tz, nx, ny, nz, tw = [column(f) for f in range(T_FIELDS)]
        sx, sy, sz, sz4, sz2, sa, se, sk = [row(f) for f in range(S_FIELDS)]
        delta_x = tx - sx
        delta_y = ty - sy
        delta_z = tz - sz
        level = delta_x * delta_x + delta_y * delta_y + sa
        near = level + delta_z * delta_z
        mirror = near + tz * sz4
        r_near = lax.rsqrt(near)
        r_mirror = lax.rsqrt(mirror)
        facing = nx * delta_x + ny * delta_y + nz * delta_z
        facing_mirror = facing + nz * sz2
        arc = level + MONIC[3]
        arc = arc * level + MONIC[2]
        arc = arc * level + MONIC[1]
        arc = arc * level + MONIC[0]
        arc = arc * level
        arc = arc * (4.0 - arc)
        arc = arc * (4.0 - arc)
        arc = arc * (4.0 - arc)
        total = (
            facing * (r_near * r_near * r_near)
            + facing_mirror * (r_mirror * r_mirror * r_mirror)
            + (arc - 2.0) * (tw * se)
        )
        tile_ref[rows, :] = (total * sk).astype(jnp.bfloat16)

    tile = tile_ref[...]
    image = lax.dot_general(
        tile, dir_ref[...], (((1,), (1,)), ((), ())), preferred_element_type=jnp.float32
    )
    back = jnp.dot(adj_ref[...], tile, preferred_element_type=jnp.float32)
    out_rows = pl.ds(pl.multiple_of(i * rows_here, rows_here), rows_here)

    @pl.when(j == 0)
    def _():
        image_ref[out_rows, :] = image

    @pl.when(j > 0)
    def _():
        image_ref[out_rows, :] += image

    @pl.when(i == 0)
    def _():
        adjoint_ref[...] = back

    @pl.when(i > 0)
    def _():
        adjoint_ref[...] += back


def pair_images(tgt, src, adj_cols, dir_cols):
    targets = tgt.shape[0]
    sources = src.shape[1]
    columns = dir_cols.shape[0]
    rows_here = min(targets, 512)
    lanes_here = min(sources, 512)
    return pl.pallas_call(
        functools.partial(pair_kernel, 16),
        grid=(sources // lanes_here, targets // rows_here),
        in_specs=[
            pl.BlockSpec((rows_here, tgt.shape[1]), lambda j, i: (i, 0)),
            pl.BlockSpec((src.shape[0], lanes_here), lambda j, i: (0, j)),
            pl.BlockSpec((columns, rows_here), lambda j, i: (0, i)),
            pl.BlockSpec((columns, lanes_here), lambda j, i: (0, j)),
        ],
        out_specs=[
            pl.BlockSpec((targets, columns), lambda j, i: (0, 0)),
            pl.BlockSpec((columns, lanes_here), lambda j, i: (0, j)),
        ],
        out_shape=[
            jax.ShapeDtypeStruct((targets, columns), jnp.float32),
            jax.ShapeDtypeStruct((columns, sources), jnp.float32),
        ],
        scratch_shapes=[pltpu.VMEM((rows_here, lanes_here), jnp.bfloat16)],
        name="pair_images",
    )(tgt, src, adj_cols, dir_cols)


MESH = pl.DeviceIdType.MESH


def others(nrow, ncol):
    r, c = lax.axis_index("row"), lax.axis_index("col")
    along_col = [(r, lax.rem(c + k, ncol)) for k in range(1, ncol)]
    along_row = [(lax.rem(r + k, nrow), c) for k in range(1, nrow)]
    return r, c, along_col, along_row


def greet(peers):
    barrier = pltpu.get_barrier_semaphore()
    for peer in peers:
        pl.semaphore_signal(barrier, inc=1, device_id=peer, device_id_type=MESH)
    pl.semaphore_wait(barrier, len(peers))


def send(source, target, send_sem, recv_sem, slot, peer):
    copy = pltpu.make_async_remote_copy(
        src_ref=source,
        dst_ref=target,
        send_sem=send_sem.at[slot],
        recv_sem=recv_sem.at[slot],
        device_id=peer,
        device_id_type=MESH,
    )
    copy.start()
    return copy


def gather_kernel(
    nrow,
    ncol,
    tgt_ref,
    adj_ref,
    src_ref,
    dir_ref,
    tgt_all,
    adj_all,
    src_all,
    dir_all,
    send_sem,
    recv_sem,
    own_sem,
):
    r, c, along_col, along_row = others(nrow, ncol)
    greet(along_col + along_row)
    copies = []
    for peer in along_row:
        for source, target in ((dir_ref, dir_all), (src_ref, src_all)):
            copies.append(send(source, target.at[r], send_sem, recv_sem, len(copies), peer))
    for peer in along_col:
        for source, target in ((adj_ref, adj_all), (tgt_ref, tgt_all)):
            copies.append(send(source, target.at[c], send_sem, recv_sem, len(copies), peer))
    mine = (
        (tgt_ref, tgt_all.at[c]),
        (adj_ref, adj_all.at[c]),
        (src_ref, src_all.at[r]),
        (dir_ref, dir_all.at[r]),
    )
    kept = []
    for slot, (source, target) in enumerate(mine):
        copy = pltpu.make_async_copy(source, target, own_sem.at[slot])
        copy.start()
        kept.append(copy)
    for copy in kept + copies:
        copy.wait()


def gather_all(nrow, ncol, tgt, adj, src, direct):
    count = 2 * (nrow + ncol - 2)
    anywhere = pl.BlockSpec(memory_space=pl.ANY)
    return pl.pallas_call(
        functools.partial(gather_kernel, nrow, ncol),
        in_specs=[anywhere] * 4,
        out_specs=[anywhere] * 4,
        out_shape=[
            jax.ShapeDtypeStruct((number,) + x.shape, x.dtype)
            for number, x in ((ncol, tgt), (ncol, adj), (nrow, src), (nrow, direct))
        ],
        scratch_shapes=[
            pltpu.SemaphoreType.DMA((count,)),
            pltpu.SemaphoreType.DMA((count,)),
            pltpu.SemaphoreType.DMA((4,)),
        ],
        compiler_params=pltpu.CompilerParams(collective_id=0, has_side_effects=True),
        name="gather_all",
    )(tgt, adj, src, direct)


def density_kernel(
    nrow, ncol, tgt_ref, src_ref, mine_ref, every_ref, got_tgt, got_src, send_sem, recv_sem
):
    r, c, along_col, along_row = others(nrow, ncol)
    greet(along_col + along_row)
    copies = []
    for k, peer in enumerate(along_col):
        copies.append(
            send(tgt_ref.at[peer[1]], got_tgt.at[k], send_sem, recv_sem, len(copies), peer)
        )
    for k, peer in enumerate(along_row):
        copies.append(
            send(src_ref.at[peer[0]], got_src.at[k], send_sem, recv_sem, len(copies), peer)
        )
    total = tgt_ref[c] + src_ref[r]
    for copy in copies:
        copy.wait()
    for k in range(ncol - 1):
        total = total + got_tgt[k]
    for k in range(nrow - 1):
        total = total + got_src[k]
    mine_ref[...] = total
    every_ref[r, c] = total
    first = len(copies)
    spread = [
        send(every_ref.at[r, c], every_ref.at[r, c], send_sem, recv_sem, first + k, peer)
        for k, peer in enumerate(along_col)
    ]
    for copy in spread:
        copy.wait()
    first = first + len(spread)
    spread = [
        send(every_ref.at[r], every_ref.at[r], send_sem, recv_sem, first + k, peer)
        for k, peer in enumerate(along_row)
    ]
    for copy in spread:
        copy.wait()


def sum_densities(nrow, ncol, tgt, src):
    size = tgt.shape[-1]
    count = 2 * (nrow + ncol - 2)
    vmem = pl.BlockSpec(memory_space=pltpu.VMEM)
    return pl.pallas_call(
        functools.partial(density_kernel, nrow, ncol),
        in_specs=[vmem] * 2,
        out_specs=[vmem] * 2,
        out_shape=[
            jax.ShapeDtypeStruct((1, size), jnp.float32),
            jax.ShapeDtypeStruct((nrow, ncol, 1, size), jnp.float32),
        ],
        scratch_shapes=[
            pltpu.VMEM((ncol - 1, 1, size), jnp.float32),
            pltpu.VMEM((nrow - 1, 1, size), jnp.float32),
            pltpu.SemaphoreType.DMA((count,)),
            pltpu.SemaphoreType.DMA((count,)),
        ],
        compiler_params=pltpu.CompilerParams(collective_id=1, has_side_effects=True),
        name="sum_densities",
    )(tgt, src)


def patch_kernel(nrow, ncol, part_ref, out_ref, got, sums, send_sem, recv_sem):
    r, c, along_col, along_row = others(nrow, ncol)
    greet(along_col + along_row)
    copies = [
        send(part_ref.at[peer[0]], got.at[k], send_sem, recv_sem, k, peer)
        for k, peer in enumerate(along_row)
    ]
    total = part_ref[r]
    for copy in copies:
        copy.wait()
    for k in range(nrow - 1):
        total = total + got[k]
    sums[c] = total
    first = len(copies)
    copies = [
        send(sums.at[c], sums.at[c], send_sem, recv_sem, first + k, peer)
        for k, peer in enumerate(along_col)
    ]
    for copy in copies:
        copy.wait()
    total = sums[0]
    for k in range(1, ncol):
        total = total + sums[k]
    out_ref[...] = total


def sum_patches(nrow, ncol, part):
    count = nrow + ncol - 2
    vmem = pl.BlockSpec(memory_space=pltpu.VMEM)
    return pl.pallas_call(
        functools.partial(patch_kernel, nrow, ncol),
        in_specs=[vmem],
        out_specs=vmem,
        out_shape=jax.ShapeDtypeStruct(part.shape[1:], jnp.float32),
        scratch_shapes=[
            pltpu.VMEM((nrow - 1,) + part.shape[1:], jnp.float32),
            pltpu.VMEM((ncol,) + part.shape[1:], jnp.float32),
            pltpu.SemaphoreType.DMA((count,)),
            pltpu.SemaphoreType.DMA((count,)),
        ],
        compiler_params=pltpu.CompilerParams(collective_id=2, has_side_effects=True),
        name="sum_patches",
    )(part)


def on_device(
    nrow,
    ncol,
    positions,
    normals,
    areas,
    direct,
    adjoint,
    spline,
    block_lists,
    patch_counts,
    patch_owner,
):
    length = math.sqrt(SQ_SCALE)
    depth = 0.5 * (positions[2] - 1.2)
    grow = jnp.exp(wave_number * depth)
    flat = length * positions[:2]
    deep = (length * depth)[None]
    size = positions.shape[1]
    tgt_fields = jnp.concatenate(
        [
            flat,
            deep,
            normals,
            ((wave_number / SQ_SCALE) * normals[2] * grow)[None],
            jnp.zeros_like(deep),
        ],
        axis=0,
    )
    src_fields = jnp.concatenate(
        [
            flat,
            deep,
            4.0 * deep,
            2.0 * deep,
            (SQ_SCALE * areas)[None],
            grow[None],
            ((SQ_SCALE * inv_four_pi) * areas)[None],
        ],
        axis=0,
    )
    tgt_all, adj_all, src_all, dir_all = gather_all(
        nrow, ncol, tgt_fields, adjoint.T, src_fields, direct.T
    )

    def beside(chunks):
        return jnp.swapaxes(chunks, 0, 1).reshape(chunks.shape[1], -1)

    tgt = jnp.swapaxes(tgt_all, 1, 2).reshape(-1, tgt_all.shape[1])
    src = jnp.repeat(beside(src_all), 8, axis=0)
    adj_cols = beside(adj_all)
    dir_cols = beside(dir_all)
    image, back = pair_images(tgt, src, adj_cols, dir_cols)
    dens_tgt = jnp.sum(adj_cols.astype(jnp.float32) * image.T, axis=0)
    dens_src = jnp.sum(dir_cols.astype(jnp.float32) * back, axis=0)
    densities, every_density = sum_densities(
        nrow, ncol, dens_tgt.reshape(ncol, 1, size), dens_src.reshape(nrow, 1, size)
    )
    densities = densities.reshape(size)
    blocks = every_density.reshape(NBLK, BPAN)
    ends = jnp.cumsum(patch_counts)
    starts = ends - patch_counts
    block_ids = jnp.arange(NBLK, dtype=jnp.int32)
    inside = (
        (starts[:, None] <= block_ids[None, :]) & (block_ids[None, :] < ends[:, None])
    ).astype(jnp.float32)
    owners = (patch_owner[None, :] == jnp.arange(NPATCH, dtype=jnp.int32)[:, None]).astype(
        jnp.float32
    )
    owned = jnp.dot(owners, inside, precision=lax.Precision.HIGHEST)
    holder = lax.axis_index(("row", "col"))
    listed = jnp.any(block_lists == holder, axis=1).astype(jnp.float32)
    weights = owned * listed[None, :]
    gathered = jnp.dot(weights, blocks, precision=lax.Precision.HIGHEST)
    contrib = jnp.dot(gathered, spline[0].astype(jnp.float32), precision=lax.Precision.HIGHEST)
    patch_grad = sum_patches(nrow, ncol, contrib.reshape(nrow, -1, contrib.shape[1]))
    return (densities, patch_grad)


def solution(mesh):
    placed = (
        P(None, ("row", "col")),
        P(None, ("row", "col")),
        P(("row", "col")),
        P(("row", "col"), None),
        P(("row", "col"), None),
        P(("row", "col"), None, None),
        P(),
        P(),
        P(),
    )
    return jax.shard_map(
        functools.partial(on_device, mesh.shape["row"], mesh.shape["col"]),
        mesh=mesh,
        in_specs=placed,
        out_specs=(P(("row", "col")), P("row", None)),
        check_vma=False,
    )
```

```python
import functools
import math

import jax
import jax.numpy as jnp
from jax import lax
from jax.experimental import pallas as pl
from jax.experimental.pallas import tpu as pltpu
from jax.sharding import PartitionSpec as P

BPAN = 256
NPATCH = 64
NBLK = 128

wave_number = 6.0
inv_four_pi = 0.07957747154594767

HALF_ANGLE = (
    0.5624999387637301,
    -0.026367050589663217,
    0.0004942961270241117,
    -4.941951390951122e-06,
    2.8141817781696455e-08,
)
SQ_SCALE = HALF_ANGLE[-1] ** (1.0 / len(HALF_ANGLE))
MONIC = tuple(c / SQ_SCALE ** (i + 1) for i, c in enumerate(HALF_ANGLE[:-1]))

T_FIELDS = 7
S_FIELDS = 8
STEP_ROWS = 16
STRIP = 512


def pair_kernel(
    step_rows,
    strip,
    tgt_ref,
    src_ref,
    adj_ref,
    dir_ref,
    dens_tgt_ref,
    dens_src_ref,
    tgt_wide,
    src_wide,
    dir_rows,
    image_sum,
    back_sum,
    tile_ref,
):
    j = pl.program_id(0)
    i = pl.program_id(1)
    rows_here, lanes_here = tile_ref.shape
    wide = tgt_wide.shape[-1]

    @pl.when(i == 0)
    def _():
        for field in range(S_FIELDS):
            src_wide[8 * field : 8 * field + 8, :] = jnp.broadcast_to(
                src_ref[0, field : field + 1, :], (8, lanes_here)
            )
        dir_rows[...] = dir_ref[0].astype(jnp.float32).T.astype(jnp.bfloat16)
        back_sum[...] = jnp.zeros_like(back_sum)

    @pl.when(j == 0)
    def _():
        columns = tgt_ref[0].T
        for field in range(T_FIELDS):
            tgt_wide[i, field] = jnp.broadcast_to(
                columns[:, field : field + 1], (rows_here, wide)
            )
        image_sum[i] = jnp.zeros(image_sum.shape[1:], jnp.float32)

    def column(field, start):
        part = tgt_wide[i, field, start : start + step_rows, :]
        return jnp.concatenate([part] * (strip // wide), axis=1)

    def row(field, at):
        full = src_wide[8 * field : 8 * field + 8, at : at + strip]
        return jnp.concatenate([full] * (step_rows // 8), axis=0)

    for start in range(0, rows_here, step_rows):
        for at in range(0, lanes_here, strip):
            tx, ty, tz, nx, ny, nz, tw = [column(f, start) for f in range(T_FIELDS)]
            sx, sy, sz, sz4, sz2, sa, se, sk = [row(f, at) for f in range(S_FIELDS)]
            delta_x = tx - sx
            delta_y = ty - sy
            delta_z = tz - sz
            level = delta_x * delta_x + delta_y * delta_y + sa
            near = level + delta_z * delta_z
            mirror = near + tz * sz4
            r_near = lax.rsqrt(near)
            r_mirror = lax.rsqrt(mirror)
            facing = nx * delta_x + ny * delta_y + nz * delta_z
            facing_mirror = facing + nz * sz2
            arc = level + MONIC[3]
            arc = arc * level + MONIC[2]
            arc = arc * level + MONIC[1]
            arc = arc * level + MONIC[0]
            arc = arc * level
            arc = arc * (4.0 - arc)
            arc = arc * (4.0 - arc)
            arc = arc * (4.0 - arc)
            total = (
                facing * (r_near * r_near * r_near)
                + facing_mirror * (r_mirror * r_mirror * r_mirror)
                + (arc - 2.0) * (tw * se)
            )
            tile_ref[start : start + step_rows, at : at + strip] = (total * sk).astype(
                jnp.bfloat16
            )

    tile = tile_ref[...]
    image_sum[i] += jnp.dot(tile, dir_rows[...], preferred_element_type=jnp.float32)
    back_sum[...] += jnp.dot(adj_ref[0], tile, preferred_element_type=jnp.float32)

    @pl.when(i == pl.num_programs(1) - 1)
    def _():
        dens_src_ref[0] = jnp.sum(
            dir_ref[0].astype(jnp.float32) * back_sum[...], axis=0, keepdims=True
        )

    @pl.when(j == pl.num_programs(0) - 1)
    def _():
        dens_tgt_ref[i] = jnp.sum(
            adj_ref[0].astype(jnp.float32) * image_sum[i].T, axis=0, keepdims=True
        )


def pair_densities(tgt, src, adj, direct):
    ncol, _, rows_here = tgt.shape
    nrow, _, size = src.shape
    columns = direct.shape[1]
    lanes_here = min(size, 512)
    cuts = size // lanes_here
    return pl.pallas_call(
        functools.partial(pair_kernel, min(rows_here, STEP_ROWS), min(lanes_here, STRIP)),
        grid=(nrow * cuts, ncol),
        in_specs=[
            pl.BlockSpec((1, tgt.shape[1], rows_here), lambda j, i: (i, 0, 0)),
            pl.BlockSpec((1, src.shape[1], lanes_here), lambda j, i: (j // cuts, 0, j % cuts)),
            pl.BlockSpec((1, columns, rows_here), lambda j, i: (i, 0, 0)),
            pl.BlockSpec((1, columns, lanes_here), lambda j, i: (j // cuts, 0, j % cuts)),
        ],
        out_specs=[
            pl.BlockSpec((ncol, 1, rows_here), lambda j, i: (0, 0, 0)),
            pl.BlockSpec((1, 1, lanes_here), lambda j, i: (j // cuts, 0, j % cuts)),
        ],
        out_shape=[
            jax.ShapeDtypeStruct((ncol, 1, rows_here), jnp.float32),
            jax.ShapeDtypeStruct((nrow, 1, size), jnp.float32),
        ],
        scratch_shapes=[
            pltpu.VMEM((ncol, T_FIELDS, rows_here, min(lanes_here, 128)), jnp.float32),
            pltpu.VMEM((8 * S_FIELDS, lanes_here), jnp.float32),
            pltpu.VMEM((lanes_here, columns), jnp.bfloat16),
            pltpu.VMEM((ncol, rows_here, columns), jnp.float32),
            pltpu.VMEM((columns, lanes_here), jnp.float32),
            pltpu.VMEM((rows_here, lanes_here), jnp.bfloat16),
        ],
        name="pair_images",
    )(tgt, src, adj, direct)


MESH = pl.DeviceIdType.MESH


def others(nrow, ncol):
    r, c = lax.axis_index("row"), lax.axis_index("col")
    along_col = [(r, lax.rem(c + k, ncol)) for k in range(1, ncol)]
    along_row = [(lax.rem(r + k, nrow), c) for k in range(1, nrow)]
    return r, c, along_col, along_row


def greet(peers):
    barrier = pltpu.get_barrier_semaphore()
    for peer in peers:
        pl.semaphore_signal(barrier, inc=1, device_id=peer, device_id_type=MESH)
    pl.semaphore_wait(barrier, len(peers))


def send(source, target, send_sem, recv_sem, slot, peer):
    copy = pltpu.make_async_remote_copy(
        src_ref=source,
        dst_ref=target,
        send_sem=send_sem.at[slot],
        recv_sem=recv_sem.at[slot],
        device_id=peer,
        device_id_type=MESH,
    )
    copy.start()
    return copy


def gather_kernel(
    nrow,
    ncol,
    tgt_ref,
    adj_ref,
    src_ref,
    dir_ref,
    tgt_all,
    adj_all,
    src_all,
    dir_all,
    send_sem,
    recv_sem,
    own_sem,
):
    r, c, along_col, along_row = others(nrow, ncol)
    greet(along_col + along_row)
    copies = []
    for peer in along_row:
        for source, target in ((dir_ref, dir_all), (src_ref, src_all)):
            copies.append(send(source, target.at[r], send_sem, recv_sem, len(copies), peer))
    for peer in along_col:
        for source, target in ((adj_ref, adj_all), (tgt_ref, tgt_all)):
            copies.append(send(source, target.at[c], send_sem, recv_sem, len(copies), peer))
    mine = (
        (tgt_ref, tgt_all.at[c]),
        (adj_ref, adj_all.at[c]),
        (src_ref, src_all.at[r]),
        (dir_ref, dir_all.at[r]),
    )
    kept = []
    for slot, (source, target) in enumerate(mine):
        copy = pltpu.make_async_copy(source, target, own_sem.at[slot])
        copy.start()
        kept.append(copy)
    for copy in kept + copies:
        copy.wait()


def gather_all(nrow, ncol, tgt, adj, src, direct):
    count = 2 * (nrow + ncol - 2)
    anywhere = pl.BlockSpec(memory_space=pl.ANY)
    return pl.pallas_call(
        functools.partial(gather_kernel, nrow, ncol),
        in_specs=[anywhere] * 4,
        out_specs=[anywhere] * 4,
        out_shape=[
            jax.ShapeDtypeStruct((number,) + x.shape, x.dtype)
            for number, x in ((ncol, tgt), (ncol, adj), (nrow, src), (nrow, direct))
        ],
        scratch_shapes=[
            pltpu.SemaphoreType.DMA((count,)),
            pltpu.SemaphoreType.DMA((count,)),
            pltpu.SemaphoreType.DMA((4,)),
        ],
        compiler_params=pltpu.CompilerParams(collective_id=0, has_side_effects=True),
        name="gather_all",
    )(tgt, adj, src, direct)


def density_kernel(
    nrow, ncol, tgt_ref, src_ref, mine_ref, every_ref, got_tgt, got_src, send_sem, recv_sem
):
    r, c, along_col, along_row = others(nrow, ncol)
    greet(along_col + along_row)
    copies = []
    for k, peer in enumerate(along_col):
        copies.append(
            send(tgt_ref.at[peer[1]], got_tgt.at[k], send_sem, recv_sem, len(copies), peer)
        )
    for k, peer in enumerate(along_row):
        copies.append(
            send(src_ref.at[peer[0]], got_src.at[k], send_sem, recv_sem, len(copies), peer)
        )
    total = tgt_ref[c] + src_ref[r]
    for copy in copies:
        copy.wait()
    for k in range(ncol - 1):
        total = total + got_tgt[k]
    for k in range(nrow - 1):
        total = total + got_src[k]
    mine_ref[...] = total
    every_ref[r, c] = total
    first = len(copies)
    spread = [
        send(every_ref.at[r, c], every_ref.at[r, c], send_sem, recv_sem, first + k, peer)
        for k, peer in enumerate(along_col)
    ]
    for copy in spread:
        copy.wait()
    first = first + len(spread)
    spread = [
        send(every_ref.at[r], every_ref.at[r], send_sem, recv_sem, first + k, peer)
        for k, peer in enumerate(along_row)
    ]
    for copy in spread:
        copy.wait()


def sum_densities(nrow, ncol, tgt, src):
    size = tgt.shape[-1]
    count = 2 * (nrow + ncol - 2)
    vmem = pl.BlockSpec(memory_space=pltpu.VMEM)
    return pl.pallas_call(
        functools.partial(density_kernel, nrow, ncol),
        in_specs=[vmem] * 2,
        out_specs=[vmem] * 2,
        out_shape=[
            jax.ShapeDtypeStruct((1, size), jnp.float32),
            jax.ShapeDtypeStruct((nrow, ncol, 1, size), jnp.float32),
        ],
        scratch_shapes=[
            pltpu.VMEM((ncol - 1, 1, size), jnp.float32),
            pltpu.VMEM((nrow - 1, 1, size), jnp.float32),
            pltpu.SemaphoreType.DMA((count,)),
            pltpu.SemaphoreType.DMA((count,)),
        ],
        compiler_params=pltpu.CompilerParams(collective_id=1, has_side_effects=True),
        name="sum_densities",
    )(tgt, src)


def patch_kernel(nrow, ncol, part_ref, out_ref, got, sums, send_sem, recv_sem):
    r, c, along_col, along_row = others(nrow, ncol)
    greet(along_col + along_row)
    copies = [
        send(part_ref.at[peer[0]], got.at[k], send_sem, recv_sem, k, peer)
        for k, peer in enumerate(along_row)
    ]
    total = part_ref[r]
    for copy in copies:
        copy.wait()
    for k in range(nrow - 1):
        total = total + got[k]
    sums[c] = total
    first = len(copies)
    copies = [
        send(sums.at[c], sums.at[c], send_sem, recv_sem, first + k, peer)
        for k, peer in enumerate(along_col)
    ]
    for copy in copies:
        copy.wait()
    total = sums[0]
    for k in range(1, ncol):
        total = total + sums[k]
    out_ref[...] = total


def sum_patches(nrow, ncol, part):
    count = nrow + ncol - 2
    vmem = pl.BlockSpec(memory_space=pltpu.VMEM)
    return pl.pallas_call(
        functools.partial(patch_kernel, nrow, ncol),
        in_specs=[vmem],
        out_specs=vmem,
        out_shape=jax.ShapeDtypeStruct(part.shape[1:], jnp.float32),
        scratch_shapes=[
            pltpu.VMEM((nrow - 1,) + part.shape[1:], jnp.float32),
            pltpu.VMEM((ncol,) + part.shape[1:], jnp.float32),
            pltpu.SemaphoreType.DMA((count,)),
            pltpu.SemaphoreType.DMA((count,)),
        ],
        compiler_params=pltpu.CompilerParams(collective_id=2, has_side_effects=True),
        name="sum_patches",
    )(part)


def on_device(
    nrow,
    ncol,
    positions,
    normals,
    areas,
    direct,
    adjoint,
    spline,
    block_lists,
    patch_counts,
    patch_owner,
):
    length = math.sqrt(SQ_SCALE)
    depth = 0.5 * (positions[2] - 1.2)
    grow = jnp.exp(wave_number * depth)
    flat = length * positions[:2]
    deep = (length * depth)[None]
    size = positions.shape[1]
    tgt_fields = jnp.concatenate(
        [
            flat,
            deep,
            normals,
            ((wave_number / SQ_SCALE) * normals[2] * grow)[None],
            jnp.zeros_like(deep),
        ],
        axis=0,
    )
    src_fields = jnp.concatenate(
        [
            flat,
            deep,
            4.0 * deep,
            2.0 * deep,
            (SQ_SCALE * areas)[None],
            grow[None],
            ((SQ_SCALE * inv_four_pi) * areas)[None],
        ],
        axis=0,
    )
    tgt_all, adj_all, src_all, dir_all = gather_all(
        nrow, ncol, tgt_fields, adjoint.T, src_fields, direct.T
    )
    dens_tgt, dens_src = pair_densities(tgt_all, src_all, adj_all, dir_all)
    densities, every_density = sum_densities(nrow, ncol, dens_tgt, dens_src)
    densities = densities.reshape(size)
    blocks = every_density.reshape(NBLK, BPAN)
    ends = jnp.cumsum(patch_counts)
    starts = ends - patch_counts
    block_ids = jnp.arange(NBLK, dtype=jnp.int32)
    inside = (
        (starts[:, None] <= block_ids[None, :]) & (block_ids[None, :] < ends[:, None])
    ).astype(jnp.float32)
    owners = (patch_owner[None, :] == jnp.arange(NPATCH, dtype=jnp.int32)[:, None]).astype(
        jnp.float32
    )
    owned = jnp.dot(owners, inside, precision=lax.Precision.HIGHEST)
    holder = lax.axis_index(("row", "col"))
    listed = jnp.any(block_lists == holder, axis=1).astype(jnp.float32)
    weights = owned * listed[None, :]
    gathered = jnp.dot(weights, blocks, precision=lax.Precision.HIGHEST)
    contrib = jnp.dot(gathered, spline[0].astype(jnp.float32), precision=lax.Precision.HIGHEST)
    patch_grad = sum_patches(nrow, ncol, contrib.reshape(nrow, -1, contrib.shape[1]))
    return (densities, patch_grad)


def solution(mesh):
    placed = (
        P(None, ("row", "col")),
        P(None, ("row", "col")),
        P(("row", "col")),
        P(("row", "col"), None),
        P(("row", "col"), None),
        P(("row", "col"), None, None),
        P(),
        P(),
        P(),
    )
    return jax.shard_map(
        functools.partial(on_device, mesh.shape["row"], mesh.shape["col"]),
        mesh=mesh,
        in_specs=placed,
        out_specs=(P(("row", "col")), P("row", None)),
        check_vma=False,
    )
```

```python
import functools
import math

import jax
import jax.numpy as jnp
from jax import lax
from jax.experimental import pallas as pl
from jax.experimental.pallas import tpu as pltpu
from jax.sharding import PartitionSpec as P

BPAN = 256
NPATCH = 64
NBLK = 128

wave_number = 6.0
inv_four_pi = 0.07957747154594767

PART_ANGLE = (0.049382699279181326, -0.00020320446239655373, 3.3039392806237825e-07)
SQ_SCALE = PART_ANGLE[-1] ** (1.0 / len(PART_ANGLE))
MONIC = tuple(c / SQ_SCALE ** (i + 1) for i, c in enumerate(PART_ANGLE[:-1]))

T_FIELDS = 7
S_FIELDS = 8
STEP_ROWS = 16
STRIP = 512


def pair_kernel(
    step_rows,
    strip,
    tgt_ref,
    src_ref,
    adj_ref,
    dir_ref,
    dens_tgt_ref,
    dens_src_ref,
    tgt_wide,
    src_wide,
    dir_rows,
    image_sum,
    back_sum,
    tile_ref,
):
    j = pl.program_id(0)
    i = pl.program_id(1)
    rows_here, lanes_here = tile_ref.shape
    wide = tgt_wide.shape[-1]

    @pl.when(i == 0)
    def _():
        for field in range(S_FIELDS):
            src_wide[8 * field : 8 * field + 8, :] = jnp.broadcast_to(
                src_ref[0, field : field + 1, :], (8, lanes_here)
            )
        dir_rows[...] = dir_ref[0].astype(jnp.float32).T.astype(jnp.bfloat16)
        back_sum[...] = jnp.zeros_like(back_sum)

    @pl.when(j == 0)
    def _():
        columns = tgt_ref[0].T
        for field in range(T_FIELDS):
            tgt_wide[i, field] = jnp.broadcast_to(
                columns[:, field : field + 1], (rows_here, wide)
            )
        image_sum[i] = jnp.zeros(image_sum.shape[1:], jnp.float32)

    def column(field, start):
        part = tgt_wide[i, field, start : start + step_rows, :]
        return jnp.concatenate([part] * (strip // wide), axis=1)

    def row(field, at):
        full = src_wide[8 * field : 8 * field + 8, at : at + strip]
        return jnp.concatenate([full] * (step_rows // 8), axis=0)

    for start in range(0, rows_here, step_rows):
        for at in range(0, lanes_here, strip):
            tx, ty, tz, nx, ny, nz, tw = [column(f, start) for f in range(T_FIELDS)]
            sx, sy, sz, sz4, sz2, sa, se, sk = [row(f, at) for f in range(S_FIELDS)]
            delta_x = tx - sx
            delta_y = ty - sy
            delta_z = tz - sz
            level = delta_x * delta_x + delta_y * delta_y + sa
            near = level + delta_z * delta_z
            mirror = near + tz * sz4
            r_near = lax.rsqrt(near)
            r_mirror = lax.rsqrt(mirror)
            facing = nx * delta_x + ny * delta_y + nz * delta_z
            facing_mirror = facing + nz * sz2
            arc = level + MONIC[1]
            arc = arc * level + MONIC[0]
            arc = arc * level
            for _ in range(3):
                rest = 3.0 - arc
                arc = arc * (rest * rest)
            total = (
                facing * (r_near * r_near * r_near)
                + facing_mirror * (r_mirror * r_mirror * r_mirror)
                + (arc - 2.0) * (tw * se)
            )
            tile_ref[start : start + step_rows, at : at + strip] = (total * sk).astype(
                jnp.bfloat16
            )

    tile = tile_ref[...]
    image_sum[i] += jnp.dot(tile, dir_rows[...], preferred_element_type=jnp.float32)
    back_sum[...] += jnp.dot(adj_ref[0], tile, preferred_element_type=jnp.float32)

    @pl.when(i == pl.num_programs(1) - 1)
    def _():
        dens_src_ref[0] = jnp.sum(
            dir_ref[0].astype(jnp.float32) * back_sum[...], axis=0, keepdims=True
        )

    @pl.when(j == pl.num_programs(0) - 1)
    def _():
        dens_tgt_ref[i] = jnp.sum(
            adj_ref[0].astype(jnp.float32) * image_sum[i].T, axis=0, keepdims=True
        )


def pair_densities(tgt, src, adj, direct):
    ncol, _, rows_here = tgt.shape
    nrow, _, size = src.shape
    columns = direct.shape[1]
    lanes_here = min(size, 512)
    cuts = size // lanes_here
    return pl.pallas_call(
        functools.partial(pair_kernel, min(rows_here, STEP_ROWS), min(lanes_here, STRIP)),
        grid=(nrow * cuts, ncol),
        in_specs=[
            pl.BlockSpec((1, tgt.shape[1], rows_here), lambda j, i: (i, 0, 0)),
            pl.BlockSpec((1, src.shape[1], lanes_here), lambda j, i: (j // cuts, 0, j % cuts)),
            pl.BlockSpec((1, columns, rows_here), lambda j, i: (i, 0, 0)),
            pl.BlockSpec((1, columns, lanes_here), lambda j, i: (j // cuts, 0, j % cuts)),
        ],
        out_specs=[
            pl.BlockSpec((ncol, 1, rows_here), lambda j, i: (0, 0, 0)),
            pl.BlockSpec((1, 1, lanes_here), lambda j, i: (j // cuts, 0, j % cuts)),
        ],
        out_shape=[
            jax.ShapeDtypeStruct((ncol, 1, rows_here), jnp.float32),
            jax.ShapeDtypeStruct((nrow, 1, size), jnp.float32),
        ],
        scratch_shapes=[
            pltpu.VMEM((ncol, T_FIELDS, rows_here, min(lanes_here, 128)), jnp.float32),
            pltpu.VMEM((8 * S_FIELDS, lanes_here), jnp.float32),
            pltpu.VMEM((lanes_here, columns), jnp.bfloat16),
            pltpu.VMEM((ncol, rows_here, columns), jnp.float32),
            pltpu.VMEM((columns, lanes_here), jnp.float32),
            pltpu.VMEM((rows_here, lanes_here), jnp.bfloat16),
        ],
        name="pair_images",
    )(tgt, src, adj, direct)


MESH = pl.DeviceIdType.MESH


def others(nrow, ncol):
    r, c = lax.axis_index("row"), lax.axis_index("col")
    along_col = [(r, lax.rem(c + k, ncol)) for k in range(1, ncol)]
    along_row = [(lax.rem(r + k, nrow), c) for k in range(1, nrow)]
    return r, c, along_col, along_row


def greet(peers):
    barrier = pltpu.get_barrier_semaphore()
    for peer in peers:
        pl.semaphore_signal(barrier, inc=1, device_id=peer, device_id_type=MESH)
    pl.semaphore_wait(barrier, len(peers))


def send(source, target, send_sem, recv_sem, slot, peer):
    copy = pltpu.make_async_remote_copy(
        src_ref=source,
        dst_ref=target,
        send_sem=send_sem.at[slot],
        recv_sem=recv_sem.at[slot],
        device_id=peer,
        device_id_type=MESH,
    )
    copy.start()
    return copy


def gather_kernel(
    nrow,
    ncol,
    tgt_ref,
    adj_ref,
    src_ref,
    dir_ref,
    tgt_all,
    adj_all,
    src_all,
    dir_all,
    send_sem,
    recv_sem,
    own_sem,
):
    r, c, along_col, along_row = others(nrow, ncol)
    greet(along_col + along_row)
    copies = []
    for peer in along_row:
        for source, target in ((dir_ref, dir_all), (src_ref, src_all)):
            copies.append(send(source, target.at[r], send_sem, recv_sem, len(copies), peer))
    for peer in along_col:
        for source, target in ((adj_ref, adj_all), (tgt_ref, tgt_all)):
            copies.append(send(source, target.at[c], send_sem, recv_sem, len(copies), peer))
    mine = (
        (tgt_ref, tgt_all.at[c]),
        (adj_ref, adj_all.at[c]),
        (src_ref, src_all.at[r]),
        (dir_ref, dir_all.at[r]),
    )
    kept = []
    for slot, (source, target) in enumerate(mine):
        copy = pltpu.make_async_copy(source, target, own_sem.at[slot])
        copy.start()
        kept.append(copy)
    for copy in kept + copies:
        copy.wait()


def gather_all(nrow, ncol, tgt, adj, src, direct):
    count = 2 * (nrow + ncol - 2)
    anywhere = pl.BlockSpec(memory_space=pl.ANY)
    return pl.pallas_call(
        functools.partial(gather_kernel, nrow, ncol),
        in_specs=[anywhere] * 4,
        out_specs=[anywhere] * 4,
        out_shape=[
            jax.ShapeDtypeStruct((number,) + x.shape, x.dtype)
            for number, x in ((ncol, tgt), (ncol, adj), (nrow, src), (nrow, direct))
        ],
        scratch_shapes=[
            pltpu.SemaphoreType.DMA((count,)),
            pltpu.SemaphoreType.DMA((count,)),
            pltpu.SemaphoreType.DMA((4,)),
        ],
        compiler_params=pltpu.CompilerParams(collective_id=0, has_side_effects=True),
        name="gather_all",
    )(tgt, adj, src, direct)


def density_kernel(
    nrow, ncol, tgt_ref, src_ref, mine_ref, every_ref, got_tgt, got_src, send_sem, recv_sem
):
    r, c, along_col, along_row = others(nrow, ncol)
    greet(along_col + along_row)
    copies = []
    for k, peer in enumerate(along_col):
        copies.append(
            send(tgt_ref.at[peer[1]], got_tgt.at[k], send_sem, recv_sem, len(copies), peer)
        )
    for k, peer in enumerate(along_row):
        copies.append(
            send(src_ref.at[peer[0]], got_src.at[k], send_sem, recv_sem, len(copies), peer)
        )
    total = tgt_ref[c] + src_ref[r]
    for copy in copies:
        copy.wait()
    for k in range(ncol - 1):
        total = total + got_tgt[k]
    for k in range(nrow - 1):
        total = total + got_src[k]
    mine_ref[...] = total
    every_ref[r, c] = total
    first = len(copies)
    spread = [
        send(every_ref.at[r, c], every_ref.at[r, c], send_sem, recv_sem, first + k, peer)
        for k, peer in enumerate(along_col)
    ]
    for copy in spread:
        copy.wait()
    first = first + len(spread)
    spread = [
        send(every_ref.at[r], every_ref.at[r], send_sem, recv_sem, first + k, peer)
        for k, peer in enumerate(along_row)
    ]
    for copy in spread:
        copy.wait()


def sum_densities(nrow, ncol, tgt, src):
    size = tgt.shape[-1]
    count = 2 * (nrow + ncol - 2)
    vmem = pl.BlockSpec(memory_space=pltpu.VMEM)
    return pl.pallas_call(
        functools.partial(density_kernel, nrow, ncol),
        in_specs=[vmem] * 2,
        out_specs=[vmem] * 2,
        out_shape=[
            jax.ShapeDtypeStruct((1, size), jnp.float32),
            jax.ShapeDtypeStruct((nrow, ncol, 1, size), jnp.float32),
        ],
        scratch_shapes=[
            pltpu.VMEM((ncol - 1, 1, size), jnp.float32),
            pltpu.VMEM((nrow - 1, 1, size), jnp.float32),
            pltpu.SemaphoreType.DMA((count,)),
            pltpu.SemaphoreType.DMA((count,)),
        ],
        compiler_params=pltpu.CompilerParams(collective_id=1, has_side_effects=True),
        name="sum_densities",
    )(tgt, src)


def patch_kernel(nrow, ncol, part_ref, out_ref, got, sums, send_sem, recv_sem):
    r, c, along_col, along_row = others(nrow, ncol)
    greet(along_col + along_row)
    copies = [
        send(part_ref.at[peer[0]], got.at[k], send_sem, recv_sem, k, peer)
        for k, peer in enumerate(along_row)
    ]
    total = part_ref[r]
    for copy in copies:
        copy.wait()
    for k in range(nrow - 1):
        total = total + got[k]
    sums[c] = total
    first = len(copies)
    copies = [
        send(sums.at[c], sums.at[c], send_sem, recv_sem, first + k, peer)
        for k, peer in enumerate(along_col)
    ]
    for copy in copies:
        copy.wait()
    total = sums[0]
    for k in range(1, ncol):
        total = total + sums[k]
    out_ref[...] = total


def sum_patches(nrow, ncol, part):
    count = nrow + ncol - 2
    vmem = pl.BlockSpec(memory_space=pltpu.VMEM)
    return pl.pallas_call(
        functools.partial(patch_kernel, nrow, ncol),
        in_specs=[vmem],
        out_specs=vmem,
        out_shape=jax.ShapeDtypeStruct(part.shape[1:], jnp.float32),
        scratch_shapes=[
            pltpu.VMEM((nrow - 1,) + part.shape[1:], jnp.float32),
            pltpu.VMEM((ncol,) + part.shape[1:], jnp.float32),
            pltpu.SemaphoreType.DMA((count,)),
            pltpu.SemaphoreType.DMA((count,)),
        ],
        compiler_params=pltpu.CompilerParams(collective_id=2, has_side_effects=True),
        name="sum_patches",
    )(part)


def on_device(
    nrow,
    ncol,
    positions,
    normals,
    areas,
    direct,
    adjoint,
    spline,
    block_lists,
    patch_counts,
    patch_owner,
):
    length = math.sqrt(SQ_SCALE)
    depth = 0.5 * (positions[2] - 1.2)
    grow = jnp.exp(wave_number * depth)
    flat = length * positions[:2]
    deep = (length * depth)[None]
    size = positions.shape[1]
    tgt_fields = jnp.concatenate(
        [
            flat,
            deep,
            normals,
            ((wave_number / SQ_SCALE) * normals[2] * grow)[None],
            jnp.zeros_like(deep),
        ],
        axis=0,
    )
    src_fields = jnp.concatenate(
        [
            flat,
            deep,
            4.0 * deep,
            2.0 * deep,
            (SQ_SCALE * areas)[None],
            grow[None],
            ((SQ_SCALE * inv_four_pi) * areas)[None],
        ],
        axis=0,
    )
    tgt_all, adj_all, src_all, dir_all = gather_all(
        nrow, ncol, tgt_fields, adjoint.T, src_fields, direct.T
    )
    dens_tgt, dens_src = pair_densities(tgt_all, src_all, adj_all, dir_all)
    densities, every_density = sum_densities(nrow, ncol, dens_tgt, dens_src)
    densities = densities.reshape(size)
    blocks = every_density.reshape(NBLK, BPAN)
    ends = jnp.cumsum(patch_counts)
    starts = ends - patch_counts
    block_ids = jnp.arange(NBLK, dtype=jnp.int32)
    inside = (
        (starts[:, None] <= block_ids[None, :]) & (block_ids[None, :] < ends[:, None])
    ).astype(jnp.float32)
    owners = (patch_owner[None, :] == jnp.arange(NPATCH, dtype=jnp.int32)[:, None]).astype(
        jnp.float32
    )
    owned = jnp.dot(owners, inside, precision=lax.Precision.HIGHEST)
    holder = lax.axis_index(("row", "col"))
    listed = jnp.any(block_lists == holder, axis=1).astype(jnp.float32)
    weights = owned * listed[None, :]
    gathered = jnp.dot(weights, blocks, precision=lax.Precision.HIGHEST)
    contrib = jnp.dot(gathered, spline[0].astype(jnp.float32), precision=lax.Precision.HIGHEST)
    patch_grad = sum_patches(nrow, ncol, contrib.reshape(nrow, -1, contrib.shape[1]))
    return (densities, patch_grad)


def solution(mesh):
    placed = (
        P(None, ("row", "col")),
        P(None, ("row", "col")),
        P(("row", "col")),
        P(("row", "col"), None),
        P(("row", "col"), None),
        P(("row", "col"), None, None),
        P(),
        P(),
        P(),
    )
    return jax.shard_map(
        functools.partial(on_device, mesh.shape["row"], mesh.shape["col"]),
        mesh=mesh,
        in_specs=placed,
        out_specs=(P(("row", "col")), P("row", None)),
        check_vma=False,
    )
```
